256 devices in a mesh: tm: 64 (over z_lo, x, y, core), cell: 4 (over z_hi).
Axes of the slice: x: 4, y: 4, z: 8 (z_hi: 4, z_lo: 2; z = z_hi * 2 + z_lo), core: 2. Of those that a mesh axis runs over, the one named last changes fastest.
Arguments:
- theta: float32 [3, 1024, 256], P(None, 'cell', 'tm'), may hold values from -0.6 to 0.6
- tangent: float32 [3, 1024, 256], P(None, 'cell', 'tm'), may hold values from -6 to 6
- covariates: float32 [3, 2048, 32768], P(None, 'cell', 'tm'), may hold values from -4 to 4
- counts: int32 [2048, 32768], P('cell', 'tm'), may hold values from 0 to 5
- sfirst: int32 [2048], P('cell'), may hold values from 0 to 1008, as said below
- sweight: float32 [16, 2048], P(None, 'cell'), may hold values from 0.05 to 1
- tfirst: int32 [32768], P('tm'), may hold values from 0 to 252, as said below
- tweight: float32 [4, 32768], P(None, 'tm'), may hold values from 0.05 to 1
Outputs:
- hess_vec: float32 [3, 1024, 256], P(None, 'cell', 'tm')
- gradient: float32 [3, 1024, 256], P(None, 'cell', 'tm')
The draws below stay inside these ranges and needn't reach their ends.
Inputs may be any that keep to these rules, and one draw needn't show every extreme that they name: Cell c's support block sfirst[c] to sfirst[c] + 15 lies within the basis functions (c // 512) * 256 - 16 to (c // 512 + 1) * 256 + 15. Hour h's support block tfirst[h] to tfirst[h] + 3 lies within the basis functions (h // 512) * 4 - 2 to (h // 512 + 1) * 4 + 1.
All inputs are finite; a program needn't handle non-finite values.
Results may differ from the reference program's by a relative error of at most 0.0002.
Values sent between devices are 32-bit elements; how exact they have to be, the bound alone decides.
No kernel may reach another device: no remote copies, remote signals or barrier semaphores. Data moves between devices by JAX's collectives and lax.ppermute only.
A program may use at most 64 MiB of HBM per device.

```python
import jax
import jax.numpy as jnp
from jax import lax

K = 3
S = 1024
TD = 4
WS = 16
WT = 4
HS = 16
HT = 2
CD = 512
HD = 512
TB = 256
SD = 256
NC = 2048
NH = 32768


def band_first(key, count_all, per_device, own_count, reach_back, support, limit):
    position = jnp.arange(count_all, dtype=jnp.int32)
    device = position // per_device
    lowest = jnp.maximum(device * own_count - reach_back, 0)
    highest = jnp.minimum(device * own_count + own_count + reach_back - support, limit - support)
    picked = jax.random.randint(key, (count_all,), 0, 1 << 20, dtype=jnp.int32)
    chosen = lowest + picked % (highest - lowest + 1)
    within = position % per_device
    chosen = jnp.where(within == 0, lowest, jnp.where(within == per_device - 1, highest, chosen))
    return chosen.astype(jnp.int32)


def draw_sfirst(key, part):
    return band_first(jax.random.fold_in(key, 11), NC, CD, SD, HS, WS, S)


def draw_tfirst(key, part):
    return band_first(jax.random.fold_in(key, 23), NH, HD, TD, HT, WT, TB)


def set_ends(entries, own_key, smallest, high):
    place = [jax.random.randint(jax.random.fold_in(own_key, axis), (), 0, length) for axis, length in enumerate(entries.shape)]
    longest = entries.shape.index(max(entries.shape))
    next_to = place[:longest] + [(place[longest] + 1) % entries.shape[longest]] + place[longest + 1:]
    return entries.at[tuple(place)].set(smallest).at[tuple(next_to)].set(high)


def steps_of(key, shape, shards, smallest, high):
    def one(dim, parts):
        draws = jax.random.uniform(jax.random.fold_in(jax.random.fold_in(key, 6), dim), (parts,), jnp.float32, smallest / len(shards), high / len(shards))
        return jnp.repeat(jnp.exp(draws), shape[dim] // parts).reshape((-1,) + (1,) * (len(shape) - dim - 1))

    loudness = one(*shards[0])
    for cut in shards[1:]:
        loudness = loudness * one(*cut)
    return loudness


def normal_values(stream_key, dims, deviation, most, cuts=(), held_as=jnp.bfloat16):
    drawn = deviation * jax.random.normal(stream_key, dims, jnp.float32)
    if cuts:
        drawn = drawn * steps_of(stream_key, dims, cuts, -0.22, 0.18)
    return jnp.clip(drawn, -most, most).astype(held_as)


def setup_inputs(seed: int = 0) -> dict:
    seeds = jax.random.split(jax.random.key(seed), 9)
    return {
        "theta": normal_values(seeds[0], (K, S, TB), 0.1, 0.6, ((1, 4), (2, 64)), jnp.float32),
        "tangent": normal_values(seeds[1], (K, S, TB), 1.0, 6.0, ((1, 4), (2, 64)), jnp.float32),
        "covariates": normal_values(seeds[2], (K, NC, NH), 1.0, 4.0, ((1, 4), (2, 64)), jnp.float32),
        "counts": set_ends(jax.random.randint(seeds[3], (NC, NH), 0, 6), jax.random.fold_in(seeds[3], 1), 0, 5).astype(jnp.int32),
        "sfirst": draw_sfirst(jax.random.fold_in(seeds[8], 71), 0),
        "sweight": jnp.clip(0.05 + 0.95 * jax.random.uniform(seeds[5], (WS, NC), jnp.float32) ** steps_of(seeds[5], (WS, NC), ((1, 4),), -0.2, 0.2), 0.05, 1.0),
        "tfirst": draw_tfirst(jax.random.fold_in(seeds[8], 71), 0),
        "tweight": jnp.clip(0.05 + 0.95 * jax.random.uniform(seeds[7], (WT, NH), jnp.float32) ** steps_of(seeds[7], (WT, NH), ((1, 64),), -0.2, 0.2), 0.05, 1.0),
    }


def basis_block(first, values, row_total, offset):
    diffs = jnp.arange(row_total, dtype=jnp.int32)[:, None] - (first - offset).astype(jnp.int32)[None, :]
    result = jnp.zeros((row_total, first.shape[0]), jnp.float32)
    for index in range(values.shape[0]):
        result = result + jnp.where(diffs == index, values[index][None, :], jnp.float32(0.0))
    return result


def reference(theta, tangent, covariates, counts, sfirst, sweight, tfirst, tweight):
    high = lax.Precision.HIGHEST
    space_basis = basis_block(sfirst, sweight, S, 0)
    stacked = jnp.stack([theta, tangent])
    spatial = jnp.einsum("sc,pkst->pkct", space_basis, stacked, precision=high)
    blocks = NH // HD

    def one_block(step, total):
        start = (step * HD).astype(jnp.int32)
        time_basis = basis_block(lax.dynamic_slice_in_dim(tfirst, start, HD, 0), lax.dynamic_slice_in_dim(tweight, start, HD, 1), TB, 0)
        covar_blk = lax.dynamic_slice_in_dim(covariates, start, HD, 2)
        count_blk = lax.dynamic_slice_in_dim(counts, start, HD, 1).astype(jnp.float32)
        fields = jnp.einsum("pkct,th->pkch", spatial, time_basis, precision=high)
        predictor = jnp.sum(covar_blk * fields[0], axis=0)
        tangent_pred = jnp.sum(covar_blk * fields[1], axis=0)
        rates = jnp.exp(predictor)
        weighted = jnp.stack([covar_blk * (rates * tangent_pred)[None], covar_blk * (count_blk - rates)[None]])
        return total + jnp.einsum("pkch,th->pkct", weighted, time_basis, precision=high)

    start_total = jnp.zeros((2, K, NC, TB), jnp.float32)
    time_part = lax.fori_loop(0, blocks, one_block, start_total)
    summed = jnp.einsum("sc,pkct->pkst", space_basis, time_part, precision=high)
    hess_vec = summed[0] / jnp.float32(WS * (HD // TD))
    gradient = summed[1] / jnp.float32(HD // TD)
    return hess_vec, gradient
```

```python
import jax
import jax.numpy as jnp
from jax import lax
from jax.experimental import pallas as pl
from jax.experimental.pallas import tpu as pltpu
from jax.sharding import PartitionSpec as P

HS = 16
HT = 2
F32 = jnp.float32
BF16 = jnp.bfloat16
VMEM = pl.BlockSpec(memory_space=pltpu.VMEM)


def split(x):
    high = x.astype(BF16)
    return high, (x - high.astype(F32)).astype(BF16)


def iota(shape, dim):
    return lax.broadcasted_iota(jnp.int32, shape, dim)


def dot(a, b):
    return jnp.dot(a, b, preferred_element_type=F32)


def parity(axis):
    return lax.rem(lax.axis_index(axis), 2)


def edges_kernel(theta_ref, tangent_ref, near_ref, far_ref):
    odd = parity("tm") == 1
    for p, ref in enumerate((theta_ref, tangent_ref)):
        for k in range(3):
            rows = pl.ds(2 * (3 * p + k), 2)
            low, high = ref[k, 0:HT, :], ref[k, HT : 2 * HT, :]
            near_ref[rows, :] = jnp.where(odd, low, high)
            far_ref[rows, :] = jnp.where(odd, high, low)


def widen_kernel(theta_ref, tangent_ref, near_ref, far_ref, coef_ref, one_ref, two_ref, wide):
    odd = parity("tm") == 1
    wide[...] = jnp.zeros_like(wide)
    for p, ref in enumerate((theta_ref, tangent_ref)):
        for k in range(3):
            pk = 3 * p + k
            near, far = near_ref[2 * pk : 2 * pk + 2, :], far_ref[2 * pk : 2 * pk + 2, :]
            for base in (0, 64):
                wide[base + 8 * pk : base + 8 * pk + 2, :] = jnp.where(odd, near, far)
                wide[base + 8 * pk + 2 : base + 8 * pk + 6, :] = ref[k]
                wide[base + 8 * pk + 6 : base + 8 * pk + 8, :] = jnp.where(odd, far, near)
    turned = wide[...].T
    coef_ref[...] = turned
    low, high = turned[0:HS], turned[turned.shape[0] - HS :]
    below = parity("cell") == 1
    one_ref[...] = jnp.where(below, low, high)
    two_ref[...] = jnp.where(below, high, low)


def prepare_kernel(
    coef_ref, sfirst_ref, sweight_ref, tfirst_ref, tweight_ref, shigh_ref, slow_ref, edge_ref, spread_ref, gather_ref, main_ref
):
    rows = coef_ref.shape[0]
    offset = lax.axis_index("cell") * rows - HS
    first = sfirst_ref[...] - offset
    cells = first.shape[1]
    blocks = []
    for start in range(0, rows + 2 * HS, 32):
        diffs = iota((32, cells), 0) + start - first
        total = jnp.zeros((32, cells), F32)
        for index in range(sweight_ref.shape[0]):
            total = jnp.where(diffs == index, sweight_ref[index : index + 1, :], total)
        high, low = split(total)
        shigh_ref[start : start + 32, :] = high
        slow_ref[start : start + 32, :] = low
        blocks.append(total)
    space = jnp.concatenate(blocks, axis=0)
    own_high, own_low = split(space[HS : HS + rows].T)
    edge = jnp.concatenate([space[:HS], space[HS + rows :]], axis=0)
    edge_all = jnp.concatenate([edge, edge, edge, jnp.zeros_like(edge)], axis=0).T
    edge_high, edge_low = split(edge_all)
    part = iota(edge_all.shape, 1) // 32
    edge_ref[...] = jnp.where(part == 1, edge_low.astype(F32), edge_high.astype(F32)).astype(BF16)
    coef_high, coef_low = split(coef_ref[...])
    main_ref[...] = dot(own_high, coef_high) + dot(own_low, coef_high) + dot(own_high, coef_low)

    tfirst = tfirst_ref[...] - (lax.axis_index("tm") * 4 - HT)
    hours = tfirst.shape[1]
    row = iota((192, hours), 0)
    diffs = row % 8 - tfirst
    total = jnp.zeros((192, hours), F32)
    for index in range(tweight_ref.shape[0]):
        total = jnp.where(diffs == index, tweight_ref[index : index + 1, :], total)
    high, low = split(total)
    high, low = high.astype(F32), low.astype(F32)
    spread = jnp.where(row < 128, high, low)
    owner = (row // 8) % 8
    turned = jnp.where(row[:128] < 64, high[:128], low[:128]).T
    lane = (iota(turned.shape, 1) // 8) % 8
    for pk in range(6):
        mine = jnp.where(owner == pk, spread, 0.0).astype(BF16)
        back = jnp.where(lane == pk, turned, 0.0).astype(BF16)
        for j in range(4):
            spread_ref[j, :, 128 * pk : 128 * pk + 128] = mine[:, 128 * j : 128 * j + 128]
            gather_ref[j, 128 * pk : 128 * pk + 128, :] = back[128 * j : 128 * j + 128, :]


def main_kernel(
    main_ref, one_ref, two_ref, edge_ref, spread_ref, gather_ref, shigh_ref, slow_ref, cov_ref, counts_ref,
    own_ref, send_one_ref, send_two_ref, fields, whigh, wlow,
):
    odd = parity("cell") == 1
    one, two = one_ref[...], two_ref[...]
    halo = jnp.concatenate([jnp.where(odd, one, two), jnp.where(odd, two, one)], axis=0)
    halo_high, halo_low = split(halo)
    stacked = jnp.concatenate([halo_high, halo_high, halo_low, jnp.zeros_like(halo_low)], axis=0)
    spatial = main_ref[...] + dot(edge_ref[...], stacked)
    high = spatial.astype(BF16).astype(F32)
    left = iota(spatial.shape, 1) < 64
    factor = jnp.concatenate(
        [jnp.where(left, high, spatial - high).astype(BF16), jnp.where(left, high, 0.0).astype(BF16)[:, :64]], axis=1
    )

    def forward(j):
        fields[j] = dot(factor, spread_ref[j])

    def weigh(j):
        lanes = slice(128 * j, 128 * j + 128)
        for start in range(0, fields.shape[1], 16):
            rows = slice(start, start + 16)
            cov = [cov_ref[k, rows, lanes] for k in range(3)]
            at = [fields[j, rows, 128 * pk : 128 * pk + 128] for pk in range(6)]
            rates = jnp.exp(cov[0] * at[0] + cov[1] * at[1] + cov[2] * at[2])
            slope = rates * (cov[0] * at[3] + cov[1] * at[4] + cov[2] * at[5])
            excess = counts_ref[rows, lanes].astype(F32) - rates
            for p, value in enumerate((slope, excess)):
                for k in range(3):
                    columns = slice(128 * (3 * p + k), 128 * (3 * p + k) + 128)
                    upper, lower = split(cov[k] * value)
                    whigh[j, rows, columns] = upper
                    wlow[j, rows, columns] = lower

    def back(j):
        return dot(whigh[j], gather_ref[j]) + dot(wlow[j], gather_ref[j])

    forward(0)
    total = jnp.zeros(spatial.shape, F32)
    for j in range(4):
        if j < 3:
            forward(j + 1)
        weigh(j)
        if j > 0:
            total = total + back(j - 1)
    total = total + back(3)
    total = total + pltpu.roll(total, 64, 1)
    total_high, total_low = split(total)
    summed = dot(shigh_ref[...], total_high) + dot(slow_ref[...], total_high) + dot(shigh_ref[...], total_low)
    count = own_ref.shape[0]
    own_ref[...] = summed[HS : HS + count]
    low, high = summed[:HS], summed[HS + count :]
    send_one_ref[...] = jnp.where(odd, low, high)
    send_two_ref[...] = jnp.where(odd, high, low)


def turn_kernel(own_ref, one_ref, two_ref, wide_ref, near_ref, far_ref):
    below = parity("cell") == 1
    one, two = one_ref[...], two_ref[...]
    count = own_ref.shape[0]
    low = own_ref[:HS] + jnp.where(below, one, two)
    high = own_ref[count - HS :] + jnp.where(below, two, one)
    turned = jnp.concatenate([low, own_ref[HS : count - HS], high], axis=0).T
    wide_ref[...] = turned[:48]
    odd = parity("tm") == 1
    for pk in range(6):
        low, high = turned[8 * pk : 8 * pk + 2], turned[8 * pk + 6 : 8 * pk + 8]
        near_ref[2 * pk : 2 * pk + 2, :] = jnp.where(odd, low, high)
        far_ref[2 * pk : 2 * pk + 2, :] = jnp.where(odd, high, low)


def finish_kernel(wide_ref, near_ref, far_ref, hess_ref, grad_ref, *, scales):
    odd = parity("tm") == 1
    for p, ref in enumerate((hess_ref, grad_ref)):
        for k in range(3):
            pk = 3 * p + k
            near, far = near_ref[2 * pk : 2 * pk + 2, :], far_ref[2 * pk : 2 * pk + 2, :]
            ref[k, 0:2, :] = (wide_ref[8 * pk + 2 : 8 * pk + 4, :] + jnp.where(odd, near, far)) * scales[p]
            ref[k, 2:4, :] = (wide_ref[8 * pk + 4 : 8 * pk + 6, :] + jnp.where(odd, far, near)) * scales[p]


def call(kernel, outs, scratch=(), **kwargs):
    return pl.pallas_call(
        kernel,
        out_shape=tuple(jax.ShapeDtypeStruct(s, d) for s, d in outs),
        out_specs=tuple(VMEM for _ in outs),
        scratch_shapes=list(scratch),
        **kwargs,
    )


def swap(value, axis, pairs):
    return lax.ppermute(value, axis, [(a, b) for a, b in pairs] + [(b, a) for a, b in pairs])


def body(theta, tangent, covariates, counts, sfirst, sweight, tfirst, tweight):
    hours = counts.shape[1]
    rows = theta.shape[1]
    cells = counts.shape[0]
    periods, regions = lax.axis_size("tm"), lax.axis_size("cell")

    def over_tm(near, far):
        return (
            swap(near, "tm", [(t, t + 1) for t in range(0, periods, 2)]),
            swap(far, "tm", [(t, t + 1) for t in range(1, periods - 1, 2)]),
        )

    def over_cell(one, two):
        second = swap(two, "cell", [(c, c + 1) for c in range(1, regions - 1, 2)])
        return swap(one, "cell", [(c, c + 1) for c in range(0, regions, 2)]), second

    theta_t, tangent_t = jnp.swapaxes(theta, 1, 2), jnp.swapaxes(tangent, 1, 2)
    strip = ((12, rows), F32)
    band = ((HS, 128), F32)
    near, far = over_tm(*call(edges_kernel, [strip, strip])(theta_t, tangent_t))
    coef, one, two = call(widen_kernel, [((rows, 128), F32), band, band], [pltpu.VMEM((128, rows), F32)])(
        theta_t, tangent_t, near, far
    )
    one, two = over_cell(one, two)
    span = rows + 2 * HS
    shigh, slow, edge, spread, gather, main = call(
        prepare_kernel,
        [
            ((span, cells), BF16), ((span, cells), BF16), ((cells, 128), BF16),
            ((4, 192, 768), BF16), ((4, 768, 128), BF16), ((cells, 128), F32),
        ],
    )(coef, sfirst[None], sweight, tfirst[None], tweight)
    own, one, two = call(
        main_kernel,
        [((rows, 128), F32), band, band],
        [pltpu.VMEM((4, cells, 768), F32), pltpu.VMEM((4, cells, 768), BF16), pltpu.VMEM((4, cells, 768), BF16)],
    )(main, one, two, edge, spread, gather, shigh, slow, covariates, counts)
    one, two = over_cell(one, two)
    wide, near, far = call(turn_kernel, [((48, rows), F32), strip, strip])(own, one, two)
    near, far = over_tm(near, far)
    scales = (1.0 / (16 * (hours // 4)), 1.0 / (hours // 4))

    def last(*refs):
        finish_kernel(*refs, scales=scales)

    hess, grad = call(last, [((3, 4, rows), F32)] * 2)(wide, near, far)
    return jnp.swapaxes(hess, 1, 2), jnp.swapaxes(grad, 1, 2)


def solution(mesh):
    return jax.shard_map(
        body,
        mesh=mesh,
        in_specs=(
            P(None, "cell", "tm"),
            P(None, "cell", "tm"),
            P(None, "cell", "tm"),
            P("cell", "tm"),
            P("cell"),
            P(None, "cell"),
            P("tm"),
            P(None, "tm"),
        ),
        out_specs=(P(None, "cell", "tm"), P(None, "cell", "tm")),
        check_vma=False,
    )
```

```python
import jax
import jax.numpy as jnp
from jax import lax
from jax.experimental import pallas as pl
from jax.experimental.pallas import tpu as pltpu
from jax.sharding import PartitionSpec as P

HS = 16
HT = 2
F32 = jnp.float32
BF16 = jnp.bfloat16
VMEM = pl.BlockSpec(memory_space=pltpu.VMEM)


def split(x):
    high = x.astype(BF16)
    return high, (x - high.astype(F32)).astype(BF16)


def iota(shape, dim):
    return lax.broadcasted_iota(jnp.int32, shape, dim)


def dot(a, b):
    return jnp.dot(a, b, preferred_element_type=F32)


def parity(axis):
    return lax.rem(lax.axis_index(axis), 2)


def load_kernel(*refs):
    sources, held, (near_ref, far_ref, sems) = refs[:6], refs[6:12], refs[12:]
    copies = [pltpu.make_async_copy(a, b, sems.at[i]) for i, (a, b) in enumerate(zip(sources, held))]
    for copy in copies:
        copy.start()
    for copy in copies:
        copy.wait()
    odd = parity("tm") == 1
    for p, ref in enumerate(held[:2]):
        for k in range(3):
            rows = pl.ds(2 * (3 * p + k), 2)
            low, high = ref[k, 0:HT, :], ref[k, HT : 2 * HT, :]
            near_ref[rows, :] = jnp.where(odd, low, high)
            far_ref[rows, :] = jnp.where(odd, high, low)


def widen_kernel(theta_ref, tangent_ref, near_ref, far_ref, after_ref, coef_ref, one_ref, two_ref, wide):
    odd = parity("tm") == 1
    wide[...] = jnp.zeros_like(wide)
    for p, ref in enumerate((theta_ref, tangent_ref)):
        for k in range(3):
            pk = 3 * p + k
            near, far = near_ref[2 * pk : 2 * pk + 2, :], far_ref[2 * pk : 2 * pk + 2, :]
            for base in (0, 64):
                wide[base + 8 * pk : base + 8 * pk + 2, :] = jnp.where(odd, near, far)
                wide[base + 8 * pk + 2 : base + 8 * pk + 6, :] = ref[k]
                wide[base + 8 * pk + 6 : base + 8 * pk + 8, :] = jnp.where(odd, far, near)
    turned = wide[...].T
    coef_ref[...] = turned
    low, high = turned[0:HS], turned[turned.shape[0] - HS :]
    below = parity("cell") == 1
    one_ref[...] = jnp.where(below, low, high)
    two_ref[...] = jnp.where(below, high, low)


def basis_kernel(
    sfirst_ref, sweight_ref, tfirst_ref, tweight_ref, cov_any, counts_any,
    shigh_ref, slow_ref, turned_high_ref, turned_low_ref, edge_ref, spread_ref, gather_ref, cov_ref, counts_ref, sems,
):
    copies = (pltpu.make_async_copy(cov_any, cov_ref, sems.at[0]), pltpu.make_async_copy(counts_any, counts_ref, sems.at[1]))
    for copy in copies:
        copy.start()
    rows = turned_high_ref.shape[1]
    offset = lax.axis_index("cell") * rows - HS
    first = sfirst_ref[...] - offset
    cells = first.shape[1]
    blocks = []
    for start in range(0, rows + 2 * HS, 32):
        diffs = iota((32, cells), 0) + start - first
        total = jnp.zeros((32, cells), F32)
        for index in range(sweight_ref.shape[0]):
            total = jnp.where(diffs == index, sweight_ref[index : index + 1, :], total)
        high, low = split(total)
        shigh_ref[start : start + 32, :] = high
        slow_ref[start : start + 32, :] = low
        blocks.append(total)
    space = jnp.concatenate(blocks, axis=0)
    turned_high_ref[...], turned_low_ref[...] = split(space[HS : HS + rows].T)
    edge = jnp.concatenate([space[:HS], space[HS + rows :]], axis=0)
    edge_all = jnp.concatenate([edge, edge, edge, jnp.zeros_like(edge)], axis=0).T
    edge_high, edge_low = split(edge_all)
    part = iota(edge_all.shape, 1) // 32
    edge_ref[...] = jnp.where(part == 1, edge_low.astype(F32), edge_high.astype(F32)).astype(BF16)

    tfirst = tfirst_ref[...] - (lax.axis_index("tm") * 4 - HT)
    hours = tfirst.shape[1]
    row = iota((192, hours), 0)
    diffs = row % 8 - tfirst
    total = jnp.zeros((192, hours), F32)
    for index in range(tweight_ref.shape[0]):
        total = jnp.where(diffs == index, tweight_ref[index : index + 1, :], total)
    high, low = split(total)
    high, low = high.astype(F32), low.astype(F32)
    spread = jnp.where(row < 128, high, low)
    owner = (row // 8) % 8
    turned = jnp.where(row[:128] < 64, high[:128], low[:128]).T
    lane = (iota(turned.shape, 1) // 8) % 8
    for pk in range(6):
        mine = jnp.where(owner == pk, spread, 0.0).astype(BF16)
        back = jnp.where(lane == pk, turned, 0.0).astype(BF16)
        for j in range(4):
            spread_ref[j, :, 128 * pk : 128 * pk + 128] = mine[:, 128 * j : 128 * j + 128]
            gather_ref[j, 128 * pk : 128 * pk + 128, :] = back[128 * j : 128 * j + 128, :]
    for copy in copies:
        copy.wait()


def inner_kernel(coef_ref, high_ref, low_ref, main_ref):
    coef_high, coef_low = split(coef_ref[...])
    main_ref[...] = dot(high_ref[...], coef_high) + dot(low_ref[...], coef_high) + dot(high_ref[...], coef_low)


def main_kernel(
    main_ref, one_ref, two_ref, edge_ref, spread_ref, gather_ref, shigh_ref, slow_ref, cov_ref, counts_ref,
    own_ref, send_one_ref, send_two_ref, fields, whigh, wlow,
):
    odd = parity("cell") == 1
    one, two = one_ref[...], two_ref[...]
    halo = jnp.concatenate([jnp.where(odd, one, two), jnp.where(odd, two, one)], axis=0)
    halo_high, halo_low = split(halo)
    stacked = jnp.concatenate([halo_high, halo_high, halo_low, jnp.zeros_like(halo_low)], axis=0)
    spatial = main_ref[...] + dot(edge_ref[...], stacked)
    high = spatial.astype(BF16).astype(F32)
    left = iota(spatial.shape, 1) < 64
    factor = jnp.concatenate(
        [jnp.where(left, high, spatial - high).astype(BF16), jnp.where(left, high, 0.0).astype(BF16)[:, :64]], axis=1
    )

    def forward(j):
        fields[j] = dot(factor, spread_ref[j])

    def weigh(j):
        lanes = slice(128 * j, 128 * j + 128)
        for start in range(0, fields.shape[1], 16):
            rows = slice(start, start + 16)
            cov = [cov_ref[k, rows, lanes] for k in range(3)]
            at = [fields[j, rows, 128 * pk : 128 * pk + 128] for pk in range(6)]
            rates = jnp.exp(cov[0] * at[0] + cov[1] * at[1] + cov[2] * at[2])
            slope = rates * (cov[0] * at[3] + cov[1] * at[4] + cov[2] * at[5])
            excess = counts_ref[rows, lanes].astype(F32) - rates
            for p, value in enumerate((slope, excess)):
                for k in range(3):
                    columns = slice(128 * (3 * p + k), 128 * (3 * p + k) + 128)
                    upper, lower = split(cov[k] * value)
                    whigh[j, rows, columns] = upper
                    wlow[j, rows, columns] = lower

    def back(j):
        return dot(whigh[j], gather_ref[j]) + dot(wlow[j], gather_ref[j])

    forward(0)
    total = jnp.zeros(spatial.shape, F32)
    for j in range(4):
        if j < 3:
            forward(j + 1)
        weigh(j)
        if j > 0:
            total = total + back(j - 1)
    total = total + back(3)
    total = total + pltpu.roll(total, 64, 1)
    total_high, total_low = split(total)
    summed = dot(shigh_ref[...], total_high) + dot(slow_ref[...], total_high) + dot(shigh_ref[...], total_low)
    count = own_ref.shape[0]
    own_ref[...] = summed[HS : HS + count]
    low, high = summed[:HS], summed[HS + count :]
    send_one_ref[...] = jnp.where(odd, low, high)
    send_two_ref[...] = jnp.where(odd, high, low)


def turn_kernel(own_ref, one_ref, two_ref, wide_ref, near_ref, far_ref):
    below = parity("cell") == 1
    one, two = one_ref[...], two_ref[...]
    count = own_ref.shape[0]
    low = own_ref[:HS] + jnp.where(below, one, two)
    high = own_ref[count - HS :] + jnp.where(below, two, one)
    turned = jnp.concatenate([low, own_ref[HS : count - HS], high], axis=0).T
    wide_ref[...] = turned[:48]
    odd = parity("tm") == 1
    for pk in range(6):
        low, high = turned[8 * pk : 8 * pk + 2], turned[8 * pk + 6 : 8 * pk + 8]
        near_ref[2 * pk : 2 * pk + 2, :] = jnp.where(odd, low, high)
        far_ref[2 * pk : 2 * pk + 2, :] = jnp.where(odd, high, low)


def finish_kernel(wide_ref, near_ref, far_ref, hess_ref, grad_ref, *, scales):
    odd = parity("tm") == 1
    for p, ref in enumerate((hess_ref, grad_ref)):
        for k in range(3):
            pk = 3 * p + k
            near, far = near_ref[2 * pk : 2 * pk + 2, :], far_ref[2 * pk : 2 * pk + 2, :]
            ref[k, 0:2, :] = (wide_ref[8 * pk + 2 : 8 * pk + 4, :] + jnp.where(odd, near, far)) * scales[p]
            ref[k, 2:4, :] = (wide_ref[8 * pk + 4 : 8 * pk + 6, :] + jnp.where(odd, far, near)) * scales[p]


def call(kernel, outs, scratch=(), final=False, apart=()):
    shape = jax.ShapeDtypeStruct if final else pltpu.VMEM

    def run(*args):
        places = [pl.BlockSpec(memory_space=pltpu.HBM) if i in apart else VMEM for i in range(len(args))]
        return pl.pallas_call(
            kernel,
            out_shape=tuple(shape(s, d) for s, d in outs),
            in_specs=places,
            out_specs=tuple(VMEM for _ in outs),
            scratch_shapes=list(scratch),
            compiler_params=pltpu.CompilerParams(vmem_limit_bytes=24 << 20),
        )(*(pltpu.with_memory_space_constraint(a, pltpu.HBM if i in apart else pltpu.VMEM) for i, a in enumerate(args)))

    return run


def swap(value, axis, pairs):
    return lax.ppermute(value, axis, [(a, b) for a, b in pairs] + [(b, a) for a, b in pairs])


def body(theta, tangent, covariates, counts, sfirst, sweight, tfirst, tweight):
    hours = counts.shape[1]
    rows = theta.shape[1]
    cells = counts.shape[0]
    periods, regions = lax.axis_size("tm"), lax.axis_size("cell")

    def over_tm(near, far):
        return (
            swap(near, "tm", [(t, t + 1) for t in range(0, periods, 2)]),
            swap(far, "tm", [(t, t + 1) for t in range(1, periods - 1, 2)]),
        )

    def over_cell(one, two):
        second = swap(two, "cell", [(c, c + 1) for c in range(1, regions - 1, 2)])
        return swap(one, "cell", [(c, c + 1) for c in range(0, regions, 2)]), second

    small = (jnp.swapaxes(theta, 1, 2), jnp.swapaxes(tangent, 1, 2), sfirst[None], sweight, tfirst[None], tweight)
    strip = ((12, rows), F32)
    band = ((HS, 128), F32)
    theta_t, tangent_t, *support, near, far = call(
        load_kernel, [(a.shape, a.dtype) for a in small] + [strip, strip], [pltpu.SemaphoreType.DMA((6,))], apart=range(6)
    )(*small)
    near, far = over_tm(near, far)
    span = rows + 2 * HS
    shigh, slow, turned_high, turned_low, edge, spread, gather, covariates, counts = call(
        basis_kernel,
        [
            ((span, cells), BF16), ((span, cells), BF16), ((cells, rows), BF16), ((cells, rows), BF16), ((cells, 128), BF16),
            ((4, 192, 768), BF16), ((4, 768, 128), BF16), (covariates.shape, F32), (counts.shape, counts.dtype),
        ],
        [pltpu.SemaphoreType.DMA((2,))],
        apart=(4, 5),
    )(*support, covariates, counts)
    coef, one, two = call(widen_kernel, [((rows, 128), F32), band, band], [pltpu.VMEM((128, rows), F32)])(
        theta_t, tangent_t, near, far, edge
    )
    one, two = over_cell(one, two)
    (main,) = call(inner_kernel, [((cells, 128), F32)])(coef, turned_high, turned_low)
    own, one, two = call(
        main_kernel,
        [((rows, 128), F32), band, band],
        [pltpu.VMEM((4, cells, 768), F32), pltpu.VMEM((4, cells, 768), BF16), pltpu.VMEM((4, cells, 768), BF16)],
    )(main, one, two, edge, spread, gather, shigh, slow, covariates, counts)
    one, two = over_cell(one, two)
    wide, near, far = call(turn_kernel, [((48, rows), F32), strip, strip])(own, one, two)
    near, far = over_tm(near, far)
    scales = (1.0 / (16 * (hours // 4)), 1.0 / (hours // 4))

    def last(*refs):
        finish_kernel(*refs, scales=scales)

    hess, grad = call(last, [((3, 4, rows), F32)] * 2, final=True)(wide, near, far)
    return jnp.swapaxes(hess, 1, 2), jnp.swapaxes(grad, 1, 2)


def solution(mesh):
    return jax.shard_map(
        body,
        mesh=mesh,
        in_specs=(
            P(None, "cell", "tm"),
            P(None, "cell", "tm"),
            P(None, "cell", "tm"),
            P("cell", "tm"),
            P("cell"),
            P(None, "cell"),
            P("tm"),
            P(None, "tm"),
        ),
        out_specs=(P(None, "cell", "tm"), P(None, "cell", "tm")),
        check_vma=False,
    )
```

```python
import jax
import jax.numpy as jnp
from jax import lax
from jax.experimental import pallas as pl
from jax.experimental.pallas import tpu as pltpu
from jax.sharding import PartitionSpec as P


HS = 16
HT = 2
F32 = jnp.float32
BF16 = jnp.bfloat16
VMEM = pl.BlockSpec(memory_space=pltpu.VMEM)


def split(x):
    high = x.astype(BF16)
    return high, (x - high.astype(F32)).astype(BF16)


def iota(shape, dim):
    return lax.broadcasted_iota(jnp.int32, shape, dim)


def dot(a, b):
    return jnp.dot(a, b, preferred_element_type=F32)


def parity(axis):
    return lax.rem(lax.axis_index(axis), 2)


def load_kernel(*refs):
    sources, held, (near_ref, far_ref, sems) = refs[:6], refs[6:12], refs[12:]
    copies = [pltpu.make_async_copy(a, b, sems.at[i]) for i, (a, b) in enumerate(zip(sources, held))]
    for copy in copies:
        copy.start()
    for copy in copies:
        copy.wait()
    odd = parity("tm") == 1
    for p, ref in enumerate(held[:2]):
        for k in range(3):
            rows = pl.ds(2 * (3 * p + k), 2)
            low, high = ref[k, 0:HT, :], ref[k, HT : 2 * HT, :]
            near_ref[rows, :] = jnp.where(odd, low, high)
            far_ref[rows, :] = jnp.where(odd, high, low)


def widen_kernel(theta_ref, tangent_ref, near_ref, far_ref, after_ref, coef_ref, one_ref, two_ref, wide):
    odd = parity("tm") == 1
    wide[...] = jnp.zeros_like(wide)
    for p, ref in enumerate((theta_ref, tangent_ref)):
        for k in range(3):
            pk = 3 * p + k
            near, far = near_ref[2 * pk : 2 * pk + 2, :], far_ref[2 * pk : 2 * pk + 2, :]
            for base in (0, 64):
                wide[base + 8 * pk : base + 8 * pk + 2, :] = jnp.where(odd, near, far)
                wide[base + 8 * pk + 2 : base + 8 * pk + 6, :] = ref[k]
                wide[base + 8 * pk + 6 : base + 8 * pk + 8, :] = jnp.where(odd, far, near)
    turned = wide[...].T
    coef_ref[...] = turned
    low, high = turned[0:HS], turned[turned.shape[0] - HS :]
    below = parity("cell") == 1
    one_ref[...] = jnp.where(below, low, high)
    two_ref[...] = jnp.where(below, high, low)


def basis_kernel(
    sfirst_ref, sweight_ref, tfirst_ref, tweight_ref, cov_any, counts_any,
    shigh_ref, slow_ref, turned_high_ref, turned_low_ref, edge_ref, spread_ref, gather_ref, cov_ref, counts_ref, sems,
):
    copies = (pltpu.make_async_copy(cov_any, cov_ref, sems.at[0]), pltpu.make_async_copy(counts_any, counts_ref, sems.at[1]))
    for copy in copies:
        copy.start()
    rows = turned_high_ref.shape[1]
    offset = lax.axis_index("cell") * rows - HS
    first = sfirst_ref[...] - offset
    cells = first.shape[1]
    blocks = []
    for start in range(0, rows + 2 * HS, 32):
        diffs = iota((32, cells), 0) + start - first
        total = jnp.zeros((32, cells), F32)
        for index in range(sweight_ref.shape[0]):
            total = jnp.where(diffs == index, sweight_ref[index : index + 1, :], total)
        high, low = split(total)
        shigh_ref[start : start + 32, :] = high
        slow_ref[start : start + 32, :] = low
        blocks.append(total)
    space = jnp.concatenate(blocks, axis=0)
    turned_high_ref[...], turned_low_ref[...] = split(space[HS : HS + rows].T)
    edge = jnp.concatenate([space[:HS], space[HS + rows :]], axis=0)
    edge_all = jnp.concatenate([edge, edge, edge, jnp.zeros_like(edge)], axis=0).T
    edge_high, edge_low = split(edge_all)
    part = iota(edge_all.shape, 1) // 32
    edge_ref[...] = jnp.where(part == 1, edge_low.astype(F32), edge_high.astype(F32)).astype(BF16)

    tfirst = tfirst_ref[...] - (lax.axis_index("tm") * 4 - HT)
    hours = tfirst.shape[1]
    row = iota((192, hours), 0)
    diffs = row % 8 - tfirst
    total = jnp.zeros((192, hours), F32)
    for index in range(tweight_ref.shape[0]):
        total = jnp.where(diffs == index, tweight_ref[index : index + 1, :], total)
    high, low = split(total)
    high, low = high.astype(F32), low.astype(F32)
    spread = jnp.where(row < 128, high, low)
    owner = (row // 8) % 8
    turned = jnp.where(row[:128] < 64, high[:128], low[:128]).T
    lane = (iota(turned.shape, 1) // 8) % 8
    for pk in range(6):
        mine = jnp.where(owner == pk, spread, 0.0).astype(BF16)
        back = jnp.where(lane == pk, turned, 0.0).astype(BF16)
        for j in range(4):
            spread_ref[j, :, 128 * pk : 128 * pk + 128] = mine[:, 128 * j : 128 * j + 128]
            gather_ref[j, 128 * pk : 128 * pk + 128, :] = back[128 * j : 128 * j + 128, :]
    for copy in copies:
        copy.wait()


def inner_kernel(coef_ref, high_ref, low_ref, main_ref):
    coef_high, coef_low = split(coef_ref[...])
    main_ref[...] = dot(high_ref[...], coef_high) + dot(low_ref[...], coef_high) + dot(high_ref[...], coef_low)


def main_kernel(
    main_ref, one_ref, two_ref, edge_ref, spread_ref, gather_ref, shigh_ref, slow_ref, cov_ref, counts_ref,
    own_ref, send_one_ref, send_two_ref, fields, whigh, wlow,
):
    odd = parity("cell") == 1
    one, two = one_ref[...], two_ref[...]
    halo = jnp.concatenate([jnp.where(odd, one, two), jnp.where(odd, two, one)], axis=0)
    halo_high, halo_low = split(halo)
    stacked = jnp.concatenate([halo_high, halo_high, halo_low, jnp.zeros_like(halo_low)], axis=0)
    spatial = main_ref[...] + dot(edge_ref[...], stacked)
    high = spatial.astype(BF16).astype(F32)
    left = iota(spatial.shape, 1) < 64
    factor = jnp.concatenate(
        [jnp.where(left, high, spatial - high).astype(BF16), jnp.where(left, high, 0.0).astype(BF16)[:, :64]], axis=1
    )

    def forward(j):
        fields[j] = dot(factor, spread_ref[j])

    def weigh(j):
        lanes = slice(128 * j, 128 * j + 128)
        for start in range(0, fields.shape[1], 16):
            rows = slice(start, start + 16)
            cov = [cov_ref[k, rows, lanes] for k in range(3)]
            at = [fields[j, rows, 128 * pk : 128 * pk + 128] for pk in range(6)]
            rates = jnp.exp(cov[0] * at[0] + cov[1] * at[1] + cov[2] * at[2])
            slope = rates * (cov[0] * at[3] + cov[1] * at[4] + cov[2] * at[5])
            excess = counts_ref[rows, lanes].astype(F32) - rates
            for p, value in enumerate((slope, excess)):
                for k in range(3):
                    columns = slice(128 * (3 * p + k), 128 * (3 * p + k) + 128)
                    upper, lower = split(cov[k] * value)
                    whigh[j, rows, columns] = upper
                    wlow[j, rows, columns] = lower

    def back(j):
        return dot(whigh[j], gather_ref[j]) + dot(wlow[j], gather_ref[j])

    forward(0)
    total = jnp.zeros(spatial.shape, F32)
    for j in range(4):
        if j < 3:
            forward(j + 1)
        weigh(j)
        if j > 0:
            total = total + back(j - 1)
    total = total + back(3)
    total = total + pltpu.roll(total, 64, 1)
    total_high, total_low = split(total)
    summed = dot(shigh_ref[...], total_high) + dot(slow_ref[...], total_high) + dot(shigh_ref[...], total_low)
    count = own_ref.shape[0]
    own_ref[...] = summed[HS : HS + count]
    low, high = summed[:HS], summed[HS + count :]
    send_one_ref[...] = jnp.where(odd, low, high)
    send_two_ref[...] = jnp.where(odd, high, low)


def turn_kernel(own_ref, one_ref, two_ref, wide_ref, near_ref, far_ref):
    below = parity("cell") == 1
    one, two = one_ref[...], two_ref[...]
    count = own_ref.shape[0]
    low = own_ref[:HS] + jnp.where(below, one, two)
    high = own_ref[count - HS :] + jnp.where(below, two, one)
    turned = jnp.concatenate([low, own_ref[HS : count - HS], high], axis=0).T
    wide_ref[...] = turned[:48]
    odd = parity("tm") == 1
    for pk in range(6):
        low, high = turned[8 * pk : 8 * pk + 2], turned[8 * pk + 6 : 8 * pk + 8]
        near_ref[2 * pk : 2 * pk + 2, :] = jnp.where(odd, low, high)
        far_ref[2 * pk : 2 * pk + 2, :] = jnp.where(odd, high, low)


def finish_kernel(wide_ref, near_ref, far_ref, hess_ref, grad_ref, *, scales):
    odd = parity("tm") == 1
    for p, ref in enumerate((hess_ref, grad_ref)):
        for k in range(3):
            pk = 3 * p + k
            near, far = near_ref[2 * pk : 2 * pk + 2, :], far_ref[2 * pk : 2 * pk + 2, :]
            ref[k, 0:2, :] = (wide_ref[8 * pk + 2 : 8 * pk + 4, :] + jnp.where(odd, near, far)) * scales[p]
            ref[k, 2:4, :] = (wide_ref[8 * pk + 4 : 8 * pk + 6, :] + jnp.where(odd, far, near)) * scales[p]


def call(kernel, outs, scratch=(), final=False, apart=()):
    shape = jax.ShapeDtypeStruct if final else pltpu.VMEM

    def run(*args):
        places = [pl.BlockSpec(memory_space=pltpu.HBM) if i in apart else VMEM for i in range(len(args))]
        return pl.pallas_call(
            kernel,
            out_shape=tuple(shape(s, d) for s, d in outs),
            in_specs=places,
            out_specs=tuple(VMEM for _ in outs),
            scratch_shapes=list(scratch),
            compiler_params=pltpu.CompilerParams(vmem_limit_bytes=24 << 20),
        )(*(pltpu.with_memory_space_constraint(a, pltpu.HBM if i in apart else pltpu.VMEM) for i, a in enumerate(args)))

    return run


def swap(value, axis, pairs):
    return lax.ppermute(value, axis, [(a, b) for a, b in pairs] + [(b, a) for a, b in pairs])


def body(theta, tangent, covariates, counts, sfirst, sweight, tfirst, tweight):
    hours = counts.shape[1]
    rows = theta.shape[1]
    cells = counts.shape[0]
    periods, regions = lax.axis_size("tm"), lax.axis_size("cell")

    def over_tm(near, far):
        far = swap(far, "tm", [(t, (t + 1) % periods) for t in range(1, periods, 2)])
        near = swap(near, "tm", [(t, t + 1) for t in range(0, periods, 2)])
        return near, far

    def over_cell(one, two):
        two = swap(two, "cell", [(c, (c + 1) % regions) for c in range(1, regions, 2)])
        one = swap(one, "cell", [(c, c + 1) for c in range(0, regions, 2)])
        return one, two

    small = (jnp.swapaxes(theta, 1, 2), jnp.swapaxes(tangent, 1, 2), sfirst[None], sweight, tfirst[None], tweight)
    strip = ((12, rows), F32)
    band = ((HS, 128), F32)
    theta_t, tangent_t, *support, near, far = call(
        load_kernel, [(a.shape, a.dtype) for a in small] + [strip, strip], [pltpu.SemaphoreType.DMA((6,))], apart=range(6)
    )(*small)
    near, far = over_tm(near, far)
    span = rows + 2 * HS
    shigh, slow, turned_high, turned_low, edge, spread, gather, covariates, counts = call(
        basis_kernel,
        [
            ((span, cells), BF16), ((span, cells), BF16), ((cells, rows), BF16), ((cells, rows), BF16), ((cells, 128), BF16),
            ((4, 192, 768), BF16), ((4, 768, 128), BF16), (covariates.shape, F32), (counts.shape, counts.dtype),
        ],
        [pltpu.SemaphoreType.DMA((2,))],
        apart=(4, 5),
    )(*support, covariates, counts)
    coef, one, two = call(widen_kernel, [((rows, 128), F32), band, band], [pltpu.VMEM((128, rows), F32)])(
        theta_t, tangent_t, near, far, edge
    )
    one, two = over_cell(one, two)
    (main,) = call(inner_kernel, [((cells, 128), F32)])(coef, turned_high, turned_low)
    own, one, two = call(
        main_kernel,
        [((rows, 128), F32), band, band],
        [pltpu.VMEM((4, cells, 768), F32), pltpu.VMEM((4, cells, 768), BF16), pltpu.VMEM((4, cells, 768), BF16)],
    )(main, one, two, edge, spread, gather, shigh, slow, covariates, counts)
    one, two = over_cell(one, two)
    wide, near, far = call(turn_kernel, [((48, rows), F32), strip, strip])(own, one, two)
    near, far = over_tm(near, far)
    scales = (1.0 / (16 * (hours // 4)), 1.0 / (hours // 4))

    def last(*refs):
        finish_kernel(*refs, scales=scales)

    hess, grad = call(last, [((3, 4, rows), F32)] * 2, final=True)(wide, near, far)
    return jnp.swapaxes(hess, 1, 2), jnp.swapaxes(grad, 1, 2)


def solution(mesh):
    return jax.shard_map(
        body,
        mesh=mesh,
        in_specs=(
            P(None, "cell", "tm"),
            P(None, "cell", "tm"),
            P(None, "cell", "tm"),
            P("cell", "tm"),
            P("cell"),
            P(None, "cell"),
            P("tm"),
            P(None, "tm"),
        ),
        out_specs=(P(None, "cell", "tm"), P(None, "cell", "tm")),
        check_vma=False,
    )
```

```python
import jax
import jax.numpy as jnp
from jax import lax
from jax.experimental import pallas as pl
from jax.experimental.pallas import tpu as pltpu
from jax.sharding import PartitionSpec as P


HS = 16
HT = 2
F32 = jnp.float32
BF16 = jnp.bfloat16
VMEM = pl.BlockSpec(memory_space=pltpu.VMEM)


def split(x):
    high = x.astype(BF16)
    return high, (x - high.astype(F32)).astype(BF16)


def iota(shape, dim):
    return lax.broadcasted_iota(jnp.int32, shape, dim)


def dot(a, b):
    return jnp.dot(a, b, preferred_element_type=F32)


def parity(axis):
    return lax.rem(lax.axis_index(axis), 2)


def load_kernel(*refs):
    sources, held, (near_ref, far_ref, sems) = refs[:6], refs[6:12], refs[12:]
    copies = [pltpu.make_async_copy(a, b, sems.at[i]) for i, (a, b) in enumerate(zip(sources, held))]
    for copy in copies:
        copy.start()
    for copy in copies:
        copy.wait()
    odd = parity("tm") == 1
    for p, ref in enumerate(held[:2]):
        for k in range(3):
            rows = pl.ds(2 * (3 * p + k), 2)
            low, high = ref[k, 0:HT, :], ref[k, HT : 2 * HT, :]
            near_ref[rows, :] = jnp.where(odd, low, high)
            far_ref[rows, :] = jnp.where(odd, high, low)


def widen_kernel(theta_ref, tangent_ref, near_ref, far_ref, after_ref, coef_ref, one_ref, two_ref, wide):
    odd = parity("tm") == 1
    wide[...] = jnp.zeros_like(wide)
    for p, ref in enumerate((theta_ref, tangent_ref)):
        for k in range(3):
            pk = 3 * p + k
            near, far = near_ref[2 * pk : 2 * pk + 2, :], far_ref[2 * pk : 2 * pk + 2, :]
            for base in (0, 64):
                wide[base + 8 * pk : base + 8 * pk + 2, :] = jnp.where(odd, near, far)
                wide[base + 8 * pk + 2 : base + 8 * pk + 6, :] = ref[k]
                wide[base + 8 * pk + 6 : base + 8 * pk + 8, :] = jnp.where(odd, far, near)
    turned = wide[...].T
    coef_ref[...] = turned
    low, high = turned[0:HS], turned[turned.shape[0] - HS :]
    below = parity("cell") == 1
    one_ref[...] = jnp.where(below, low, high)
    two_ref[...] = jnp.where(below, high, low)


def basis_kernel(
    sfirst_ref, sweight_ref, tfirst_ref, tweight_ref, cov_any, counts_any,
    shigh_ref, slow_ref, turned_high_ref, turned_low_ref, edge_ref, spread_ref, gather_ref, cov_ref, counts_ref, sems,
):
    copies = (pltpu.make_async_copy(cov_any, cov_ref, sems.at[0]), pltpu.make_async_copy(counts_any, counts_ref, sems.at[1]))
    for copy in copies:
        copy.start()
    rows = turned_high_ref.shape[1]
    offset = lax.axis_index("cell") * rows - HS
    first = sfirst_ref[...] - offset
    cells = first.shape[1]
    blocks = []
    for start in range(0, rows + 2 * HS, 32):
        diffs = iota((32, cells), 0) + start - first
        total = jnp.zeros((32, cells), F32)
        for index in range(sweight_ref.shape[0]):
            total = jnp.where(diffs == index, sweight_ref[index : index + 1, :], total)
        high, low = split(total)
        shigh_ref[start : start + 32, :] = high
        slow_ref[start : start + 32, :] = low
        blocks.append(total)
    space = jnp.concatenate(blocks, axis=0)
    turned_high_ref[...], turned_low_ref[...] = split(space[HS : HS + rows].T)
    edge = jnp.concatenate([space[:HS], space[HS + rows :]], axis=0)
    edge_all = jnp.concatenate([edge, edge, edge, jnp.zeros_like(edge)], axis=0).T
    edge_high, edge_low = split(edge_all)
    part = iota(edge_all.shape, 1) // 32
    edge_ref[...] = jnp.where(part == 1, edge_low.astype(F32), edge_high.astype(F32)).astype(BF16)

    tfirst = tfirst_ref[...] - (lax.axis_index("tm") * 4 - HT)
    hours = tfirst.shape[1]
    row = iota((192, hours), 0)
    diffs = row % 8 - tfirst
    total = jnp.zeros((192, hours), F32)
    for index in range(tweight_ref.shape[0]):
        total = jnp.where(diffs == index, tweight_ref[index : index + 1, :], total)
    high, low = split(total)
    high, low = high.astype(F32), low.astype(F32)
    spread = jnp.where(row < 128, high, low)
    owner = (row // 8) % 8
    turned = jnp.where(row[:128] < 64, high[:128], low[:128]).T
    lane = (iota(turned.shape, 1) // 8) % 8
    for pk in range(6):
        mine = jnp.where(owner == pk, spread, 0.0).astype(BF16)
        back = jnp.where(lane == pk, turned, 0.0).astype(BF16)
        for j in range(4):
            spread_ref[j, :, 128 * pk : 128 * pk + 128] = mine[:, 128 * j : 128 * j + 128]
            gather_ref[j, 128 * pk : 128 * pk + 128, :] = back[128 * j : 128 * j + 128, :]
    for copy in copies:
        copy.wait()


def inner_kernel(coef_ref, high_ref, low_ref, main_ref):
    coef_high, coef_low = split(coef_ref[...])
    main_ref[...] = dot(high_ref[...], coef_high) + dot(low_ref[...], coef_high) + dot(high_ref[...], coef_low)


def main_kernel(
    main_ref, one_ref, two_ref, edge_ref, spread_ref, gather_ref, shigh_ref, slow_ref, cov_ref, counts_ref,
    own_ref, send_one_ref, send_two_ref, fields, weighted, sums,
):
    odd = parity("cell") == 1
    one, two = one_ref[...], two_ref[...]
    halo = jnp.concatenate([jnp.where(odd, one, two), jnp.where(odd, two, one)], axis=0)
    halo_high, halo_low = split(halo)
    stacked = jnp.concatenate([halo_high, halo_high, halo_low, jnp.zeros_like(halo_low)], axis=0)
    spatial = main_ref[...] + dot(edge_ref[...], stacked)
    high = spatial.astype(BF16).astype(F32)
    left = iota(spatial.shape, 1) < 64
    factor = jnp.concatenate(
        [jnp.where(left, high, spatial - high).astype(BF16), jnp.where(left, high, 0.0).astype(BF16)[:, :64]], axis=1
    )

    cells = fields.shape[1]

    def forward(j):
        fields[j] = dot(factor, spread_ref[j])

    def weigh(j):
        lanes = slice(128 * j, 128 * j + 128)
        for start in range(0, cells, 16):
            rows = slice(start, start + 16)
            lower_rows = slice(cells + start, cells + start + 16)
            cov = [cov_ref[k, rows, lanes] for k in range(3)]
            at = [fields[j, rows, 128 * pk : 128 * pk + 128] for pk in range(6)]
            rates = jnp.exp(cov[0] * at[0] + cov[1] * at[1] + cov[2] * at[2])
            slope = rates * (cov[0] * at[3] + cov[1] * at[4] + cov[2] * at[5])
            excess = counts_ref[rows, lanes].astype(F32) - rates
            for p, value in enumerate((slope, excess)):
                for k in range(3):
                    columns = slice(128 * (3 * p + k), 128 * (3 * p + k) + 128)
                    weighted[j, rows, columns], weighted[j, lower_rows, columns] = split(cov[k] * value)

    def back(j):
        both = dot(weighted[j], gather_ref[j])
        return both[:cells] + both[cells:]

    forward(0)
    total = jnp.zeros(spatial.shape, F32)
    for j in range(4):
        if j < 3:
            forward(j + 1)
        weigh(j)
        if j > 0:
            total = total + back(j - 1)
    total = total + back(3)
    total_high, total_low = split(total)
    whole = dot(shigh_ref[...], jnp.concatenate([total_high, total_low], axis=1))
    summed = whole[:, :128] + whole[:, 128:] + dot(slow_ref[...], total_high)
    summed = summed + pltpu.roll(summed, 64, 1)
    count = own_ref.shape[0]
    own_ref[...] = summed[HS : HS + count]
    low, high = summed[:HS], summed[HS + count :]
    send_one_ref[...] = jnp.where(odd, low, high)
    send_two_ref[...] = jnp.where(odd, high, low)


def turn_kernel(own_ref, one_ref, two_ref, wide_ref, near_ref, far_ref):
    below = parity("cell") == 1
    one, two = one_ref[...], two_ref[...]
    count = own_ref.shape[0]
    low = own_ref[:HS] + jnp.where(below, one, two)
    high = own_ref[count - HS :] + jnp.where(below, two, one)
    turned = jnp.concatenate([low, own_ref[HS : count - HS], high], axis=0).T
    wide_ref[...] = turned[:48]
    odd = parity("tm") == 1
    for pk in range(6):
        low, high = turned[8 * pk : 8 * pk + 2], turned[8 * pk + 6 : 8 * pk + 8]
        near_ref[2 * pk : 2 * pk + 2, :] = jnp.where(odd, low, high)
        far_ref[2 * pk : 2 * pk + 2, :] = jnp.where(odd, high, low)


def finish_kernel(wide_ref, near_ref, far_ref, hess_ref, grad_ref, *, scales):
    odd = parity("tm") == 1
    for p, ref in enumerate((hess_ref, grad_ref)):
        for k in range(3):
            pk = 3 * p + k
            near, far = near_ref[2 * pk : 2 * pk + 2, :], far_ref[2 * pk : 2 * pk + 2, :]
            ref[k, 0:2, :] = (wide_ref[8 * pk + 2 : 8 * pk + 4, :] + jnp.where(odd, near, far)) * scales[p]
            ref[k, 2:4, :] = (wide_ref[8 * pk + 4 : 8 * pk + 6, :] + jnp.where(odd, far, near)) * scales[p]


def call(kernel, outs, scratch=(), final=False, apart=()):
    shape = jax.ShapeDtypeStruct if final else pltpu.VMEM

    def run(*args):
        places = [pl.BlockSpec(memory_space=pltpu.HBM) if i in apart else VMEM for i in range(len(args))]
        return pl.pallas_call(
            kernel,
            out_shape=tuple(shape(s, d) for s, d in outs),
            in_specs=places,
            out_specs=tuple(VMEM for _ in outs),
            scratch_shapes=list(scratch),
            compiler_params=pltpu.CompilerParams(vmem_limit_bytes=24 << 20),
        )(*(pltpu.with_memory_space_constraint(a, pltpu.HBM if i in apart else pltpu.VMEM) for i, a in enumerate(args)))

    return run


def body(theta, tangent, covariates, counts, sfirst, sweight, tfirst, tweight):
    hours = counts.shape[1]
    rows = theta.shape[1]
    cells = counts.shape[0]
    periods, regions = lax.axis_size("tm"), lax.axis_size("cell")

    every = [(t, c) for t in range(periods) for c in range(regions)]

    def swap(value, partner):
        return lax.ppermute(value, ("tm", "cell"), [(t * regions + c, partner(t, c)) for t, c in every])

    def far_of(t, c):
        if t in (0, periods - 1):
            return t * regions + (c ^ 1)
        return (t + 1 if t % 2 else t - 1) * regions + c

    def two_of(t, c):
        if c in (0, regions - 1):
            return (t ^ 1) * regions + c
        return t * regions + (c + 1 if c % 2 else c - 1)

    def over_tm(near, far):
        far = swap(far, far_of)
        near = swap(near, lambda t, c: (t ^ 1) * regions + c)
        return near, far

    def over_cell(one, two):
        two = swap(two, two_of)
        one = swap(one, lambda t, c: t * regions + (c ^ 1))
        return one, two

    small = (jnp.swapaxes(theta, 1, 2), jnp.swapaxes(tangent, 1, 2), sfirst[None], sweight, tfirst[None], tweight)
    strip = ((12, rows), F32)
    band = ((HS, 128), F32)
    theta_t, tangent_t, *support, near, far = call(
        load_kernel, [(a.shape, a.dtype) for a in small] + [strip, strip], [pltpu.SemaphoreType.DMA((6,))], apart=range(6)
    )(*small)
    near, far = over_tm(near, far)
    span = rows + 2 * HS
    shigh, slow, turned_high, turned_low, edge, spread, gather, covariates, counts = call(
        basis_kernel,
        [
            ((span, cells), BF16), ((span, cells), BF16), ((cells, rows), BF16), ((cells, rows), BF16), ((cells, 128), BF16),
            ((4, 192, 768), BF16), ((4, 768, 128), BF16), (covariates.shape, F32), (counts.shape, counts.dtype),
        ],
        [pltpu.SemaphoreType.DMA((2,))],
        apart=(4, 5),
    )(*support, covariates, counts)
    coef, one, two = call(widen_kernel, [((rows, 128), F32), band, band], [pltpu.VMEM((128, rows), F32)])(
        theta_t, tangent_t, near, far, edge
    )
    one, two = over_cell(one, two)
    (main,) = call(inner_kernel, [((cells, 128), F32)])(coef, turned_high, turned_low)
    own, one, two = call(
        main_kernel,
        [((rows, 128), F32), band, band],
        [pltpu.VMEM((4, cells, 768), F32), pltpu.VMEM((4, 2 * cells, 768), BF16), pltpu.VMEM((cells, 128), F32)],
    )(main, one, two, edge, spread, gather, shigh, slow, covariates, counts)
    one, two = over_cell(one, two)
    wide, near, far = call(turn_kernel, [((48, rows), F32), strip, strip])(own, one, two)
    near, far = over_tm(near, far)
    scales = (1.0 / (16 * (hours // 4)), 1.0 / (hours // 4))

    def last(*refs):
        finish_kernel(*refs, scales=scales)

    hess, grad = call(last, [((3, 4, rows), F32)] * 2, final=True)(wide, near, far)
    return jnp.swapaxes(hess, 1, 2), jnp.swapaxes(grad, 1, 2)


def solution(mesh):
    return jax.shard_map(
        body,
        mesh=mesh,
        in_specs=(
            P(None, "cell", "tm"),
            P(None, "cell", "tm"),
            P(None, "cell", "tm"),
            P("cell", "tm"),
            P("cell"),
            P(None, "cell"),
            P("tm"),
            P(None, "tm"),
        ),
        out_specs=(P(None, "cell", "tm"), P(None, "cell", "tm")),
        check_vma=False,
    )
```

```python
import jax
import jax.numpy as jnp
from jax import lax
from jax.experimental import pallas as pl
from jax.experimental.pallas import tpu as pltpu
from jax.sharding import PartitionSpec as P


HS = 16
HT = 2
F32 = jnp.float32
BF16 = jnp.bfloat16
VMEM = pl.BlockSpec(memory_space=pltpu.VMEM)


def split(x):
    high = x.astype(BF16)
    return high, (x - high.astype(F32)).astype(BF16)


def iota(shape, dim):
    return lax.broadcasted_iota(jnp.int32, shape, dim)


def dot(a, b):
    return jnp.dot(a, b, preferred_element_type=F32)


def fold(x):
    return jnp.where(iota((8, 128), 1) < 64, x[:8], x[8:])


def unfold(x):
    other, left = pltpu.roll(x, 64, 1), iota(x.shape, 1) < 64
    return jnp.concatenate([jnp.where(left, x, other), jnp.where(left, other, x)], axis=0)


def parity(axis):
    return lax.rem(lax.axis_index(axis), 2)


def load_kernel(*refs):
    sources, held, (near_ref, far_ref, sems) = refs[:6], refs[6:12], refs[12:]
    copies = [pltpu.make_async_copy(a, b, sems.at[i]) for i, (a, b) in enumerate(zip(sources, held))]
    for copy in copies:
        copy.start()
    for copy in copies:
        copy.wait()
    odd = parity("tm") == 1
    for p, ref in enumerate(held[:2]):
        for k in range(3):
            rows = pl.ds(2 * (3 * p + k), 2)
            low, high = ref[k, 0:HT, :], ref[k, HT : 2 * HT, :]
            near_ref[rows, :] = jnp.where(odd, low, high)
            far_ref[rows, :] = jnp.where(odd, high, low)


def widen_kernel(theta_ref, tangent_ref, near_ref, far_ref, after_ref, coef_ref, one_ref, two_ref, wide):
    odd = parity("tm") == 1
    wide[...] = jnp.zeros_like(wide)
    for p, ref in enumerate((theta_ref, tangent_ref)):
        for k in range(3):
            pk = 3 * p + k
            near, far = near_ref[2 * pk : 2 * pk + 2, :], far_ref[2 * pk : 2 * pk + 2, :]
            for base in (0, 64):
                wide[base + 8 * pk : base + 8 * pk + 2, :] = jnp.where(odd, near, far)
                wide[base + 8 * pk + 2 : base + 8 * pk + 6, :] = ref[k]
                wide[base + 8 * pk + 6 : base + 8 * pk + 8, :] = jnp.where(odd, far, near)
    turned = wide[...].T
    coef_ref[...] = turned
    low, high = fold(turned[0:HS]), fold(turned[turned.shape[0] - HS :])
    below = parity("cell") == 1
    one_ref[...] = jnp.where(below, low, high)
    two_ref[...] = jnp.where(below, high, low)


def basis_kernel(
    sfirst_ref, sweight_ref, cov_any, counts_any,
    shigh_ref, slow_ref, turned_high_ref, turned_low_ref, edge_ref, cov_ref, counts_ref, sems,
):
    copies = (pltpu.make_async_copy(cov_any, cov_ref, sems.at[0]), pltpu.make_async_copy(counts_any, counts_ref, sems.at[1]))
    for copy in copies:
        copy.start()
    rows = turned_high_ref.shape[1]
    offset = lax.axis_index("cell") * rows - HS
    first = sfirst_ref[...] - offset
    cells = first.shape[1]
    blocks = []
    for start in range(0, rows + 2 * HS, 32):
        diffs = iota((32, cells), 0) + start - first
        total = jnp.zeros((32, cells), F32)
        for index in range(sweight_ref.shape[0]):
            total = jnp.where(diffs == index, sweight_ref[index : index + 1, :], total)
        high, low = split(total)
        shigh_ref[start : start + 32, :] = high
        slow_ref[start : start + 32, :] = low
        blocks.append(total)
    space = jnp.concatenate(blocks, axis=0)
    turned_high_ref[...], turned_low_ref[...] = split(space[HS : HS + rows].T)
    edge = jnp.concatenate([space[:HS], space[HS + rows :]], axis=0)
    edge_all = jnp.concatenate([edge, edge, edge, jnp.zeros_like(edge)], axis=0).T
    edge_high, edge_low = split(edge_all)
    part = iota(edge_all.shape, 1) // 32
    edge_ref[...] = jnp.where(part == 1, edge_low.astype(F32), edge_high.astype(F32)).astype(BF16)
    for copy in copies:
        copy.wait()


def inner_kernel(coef_ref, high_ref, low_ref, tfirst_ref, tweight_ref, main_ref, spread_ref, gather_ref):
    coef_high, coef_low = split(coef_ref[...])
    main_ref[...] = dot(high_ref[...], coef_high) + dot(low_ref[...], coef_high) + dot(high_ref[...], coef_low)
    tfirst = tfirst_ref[...] - (lax.axis_index("tm") * 4 - HT)
    hours = tfirst.shape[1]
    row = iota((192, hours), 0)
    diffs = row % 8 - tfirst
    total = jnp.zeros((192, hours), F32)
    for index in range(tweight_ref.shape[0]):
        total = jnp.where(diffs == index, tweight_ref[index : index + 1, :], total)
    high, low = split(total)
    high, low = high.astype(F32), low.astype(F32)
    spread = jnp.where(row < 128, high, low)
    owner = (row // 8) % 8
    turned = jnp.where(row[:128] < 64, high[:128], low[:128]).T
    lane = (iota(turned.shape, 1) // 8) % 8
    for pk in range(6):
        mine = jnp.where(owner == pk, spread, 0.0).astype(BF16)
        back = jnp.where(lane == pk, turned, 0.0).astype(BF16)
        for j in range(4):
            spread_ref[j, :, 128 * pk : 128 * pk + 128] = mine[:, 128 * j : 128 * j + 128]
            gather_ref[j, 128 * pk : 128 * pk + 128, :] = back[128 * j : 128 * j + 128, :]


def main_kernel(
    main_ref, first_ref, two_ref, third_ref, edge_ref, spread_ref, gather_ref, shigh_ref, slow_ref, cov_ref, counts_ref,
    own_ref, send_one_ref, send_two_ref, fields, weighted, sums,
):
    odd = parity("cell") == 1
    one = jnp.where(lax.axis_index("cell") < 2, first_ref[...], third_ref[...])
    one, two = unfold(one), unfold(two_ref[...])
    halo = jnp.concatenate([jnp.where(odd, one, two), jnp.where(odd, two, one)], axis=0)
    halo_high, halo_low = split(halo)
    stacked = jnp.concatenate([halo_high, halo_high, halo_low, jnp.zeros_like(halo_low)], axis=0)
    spatial = main_ref[...] + dot(edge_ref[...], stacked)
    high = spatial.astype(BF16).astype(F32)
    left = iota(spatial.shape, 1) < 64
    factor = jnp.concatenate(
        [jnp.where(left, high, spatial - high).astype(BF16), jnp.where(left, high, 0.0).astype(BF16)[:, :64]], axis=1
    )

    cells = fields.shape[1]

    def forward(j):
        fields[j] = dot(factor, spread_ref[j])

    def weigh(j):
        lanes = slice(128 * j, 128 * j + 128)
        for start in range(0, cells, 16):
            rows = slice(start, start + 16)
            lower_rows = slice(cells + start, cells + start + 16)
            cov = [cov_ref[k, rows, lanes] for k in range(3)]
            at = [fields[j, rows, 128 * pk : 128 * pk + 128] for pk in range(6)]
            rates = jnp.exp(cov[0] * at[0] + cov[1] * at[1] + cov[2] * at[2])
            slope = rates * (cov[0] * at[3] + cov[1] * at[4] + cov[2] * at[5])
            excess = counts_ref[rows, lanes].astype(F32) - rates
            for p, value in enumerate((slope, excess)):
                for k in range(3):
                    columns = slice(128 * (3 * p + k), 128 * (3 * p + k) + 128)
                    weighted[j, rows, columns], weighted[j, lower_rows, columns] = split(cov[k] * value)

    def back(j):
        both = dot(weighted[j], gather_ref[j])
        return both[:cells] + both[cells:]

    forward(0)
    total = jnp.zeros(spatial.shape, F32)
    for j in range(4):
        if j < 3:
            forward(j + 1)
        weigh(j)
        if j > 0:
            total = total + back(j - 1)
    total = total + back(3)
    total_high, total_low = split(total)
    whole = dot(shigh_ref[...], jnp.concatenate([total_high, total_low], axis=1))
    summed = whole[:, :128] + whole[:, 128:] + dot(slow_ref[...], total_high)
    summed = summed + pltpu.roll(summed, 64, 1)
    count = own_ref.shape[0]
    own_ref[...] = summed[HS : HS + count]
    low, high = fold(summed[:HS]), fold(summed[HS + count :])
    send_one_ref[...] = jnp.where(odd, low, high)
    send_two_ref[...] = jnp.where(odd, high, low)


def turn_kernel(own_ref, one_ref, two_ref, wide_ref, near_ref, far_ref):
    below = parity("cell") == 1
    one, two = unfold(one_ref[...]), unfold(two_ref[...])
    count = own_ref.shape[0]
    low = own_ref[:HS] + jnp.where(below, one, two)
    high = own_ref[count - HS :] + jnp.where(below, two, one)
    turned = jnp.concatenate([low, own_ref[HS : count - HS], high], axis=0).T
    wide_ref[...] = turned[:48]
    odd = parity("tm") == 1
    for pk in range(6):
        low, high = turned[8 * pk : 8 * pk + 2], turned[8 * pk + 6 : 8 * pk + 8]
        near_ref[2 * pk : 2 * pk + 2, :] = jnp.where(odd, low, high)
        far_ref[2 * pk : 2 * pk + 2, :] = jnp.where(odd, high, low)


def finish_kernel(wide_ref, near_ref, far_ref, hess_ref, grad_ref, *, scales):
    odd = parity("tm") == 1
    for p, ref in enumerate((hess_ref, grad_ref)):
        for k in range(3):
            pk = 3 * p + k
            near, far = near_ref[2 * pk : 2 * pk + 2, :], far_ref[2 * pk : 2 * pk + 2, :]
            ref[k, 0:2, :] = (wide_ref[8 * pk + 2 : 8 * pk + 4, :] + jnp.where(odd, near, far)) * scales[p]
            ref[k, 2:4, :] = (wide_ref[8 * pk + 4 : 8 * pk + 6, :] + jnp.where(odd, far, near)) * scales[p]


def call(kernel, outs, scratch=(), final=False, apart=()):
    shape = jax.ShapeDtypeStruct if final else pltpu.VMEM

    def run(*args):
        places = [pl.BlockSpec(memory_space=pltpu.HBM) if i in apart else VMEM for i in range(len(args))]
        return pl.pallas_call(
            kernel,
            out_shape=tuple(shape(s, d) for s, d in outs),
            in_specs=places,
            out_specs=tuple(VMEM for _ in outs),
            scratch_shapes=list(scratch),
            compiler_params=pltpu.CompilerParams(vmem_limit_bytes=24 << 20),
        )(*(pltpu.with_memory_space_constraint(a, pltpu.HBM if i in apart else pltpu.VMEM) for i, a in enumerate(args)))

    return run


def body(theta, tangent, covariates, counts, sfirst, sweight, tfirst, tweight):
    hours = counts.shape[1]
    rows = theta.shape[1]
    cells = counts.shape[0]
    periods, regions = lax.axis_size("tm"), lax.axis_size("cell")

    every = [(t, c) for t in range(periods) for c in range(regions)]

    def swap(value, partner):
        return lax.ppermute(value, ("tm", "cell"), [(t * regions + c, partner(t, c)) for t, c in every])

    def far_of(t, c):
        if t in (0, periods - 1):
            return t * regions + (c ^ 1)
        return (t + 1 if t % 2 else t - 1) * regions + c

    def two_of(t, c):
        if c in (0, regions - 1):
            return (t ^ 1) * regions + c
        return t * regions + (c + 1 if c % 2 else c - 1)

    def over_tm(near, far):
        far = swap(far, far_of)
        near = swap(near, lambda t, c: (t ^ 1) * regions + c)
        return near, far

    def side_of(first):
        return lambda t, c: t * regions + (c ^ 1) if (c < regions // 2) == first else (t ^ 1) * regions + c

    def over_cell_in_three(one, two):
        low = swap(one, side_of(True))
        two = swap(two, two_of)
        high = swap(one, side_of(False))
        return low, two, high

    def over_cell(one, two):
        two = swap(two, two_of)
        one = swap(one, lambda t, c: t * regions + (c ^ 1))
        return one, two

    small = (jnp.swapaxes(theta, 1, 2), jnp.swapaxes(tangent, 1, 2), sfirst[None], sweight, tfirst[None], tweight)
    strip = ((12, rows), F32)
    band = ((HS // 2, 128), F32)
    theta_t, tangent_t, *support, near, far = call(
        load_kernel, [(a.shape, a.dtype) for a in small] + [strip, strip], [pltpu.SemaphoreType.DMA((6,))], apart=range(6)
    )(*small)
    near, far = over_tm(near, far)
    span = rows + 2 * HS
    shigh, slow, turned_high, turned_low, edge, covariates, counts = call(
        basis_kernel,
        [
            ((span, cells), BF16), ((span, cells), BF16), ((cells, rows), BF16), ((cells, rows), BF16), ((cells, 128), BF16),
            (covariates.shape, F32), (counts.shape, counts.dtype),
        ],
        [pltpu.SemaphoreType.DMA((2,))],
        apart=(2, 3),
    )(*support[:2], covariates, counts)
    coef, one, two = call(widen_kernel, [((rows, 128), F32), band, band], [pltpu.VMEM((128, rows), F32)])(
        theta_t, tangent_t, near, far, edge
    )
    low, two, high = over_cell_in_three(one, two)
    main, spread, gather = call(inner_kernel, [((cells, 128), F32), ((4, 192, 768), BF16), ((4, 768, 128), BF16)])(
        coef, turned_high, turned_low, *support[2:]
    )
    own, one, two = call(
        main_kernel,
        [((rows, 128), F32), band, band],
        [pltpu.VMEM((4, cells, 768), F32), pltpu.VMEM((4, 2 * cells, 768), BF16), pltpu.VMEM((cells, 128), F32)],
    )(main, low, two, high, edge, spread, gather, shigh, slow, covariates, counts)
    one, two = over_cell(one, two)
    wide, near, far = call(turn_kernel, [((48, rows), F32), strip, strip])(own, one, two)
    near, far = over_tm(near, far)
    scales = (1.0 / (16 * (hours // 4)), 1.0 / (hours // 4))

    def last(*refs):
        finish_kernel(*refs, scales=scales)

    hess, grad = call(last, [((3, 4, rows), F32)] * 2, final=True)(wide, near, far)
    return jnp.swapaxes(hess, 1, 2), jnp.swapaxes(grad, 1, 2)


def solution(mesh):
    return jax.shard_map(
        body,
        mesh=mesh,
        in_specs=(
            P(None, "cell", "tm"),
            P(None, "cell", "tm"),
            P(None, "cell", "tm"),
            P("cell", "tm"),
            P("cell"),
            P(None, "cell"),
            P("tm"),
            P(None, "tm"),
        ),
        out_specs=(P(None, "cell", "tm"), P(None, "cell", "tm")),
        check_vma=False,
    )
```

```python
import jax
import jax.numpy as jnp
from jax import lax
from jax.experimental import pallas as pl
from jax.experimental.pallas import tpu as pltpu
from jax.sharding import PartitionSpec as P


HS = 16
HT = 2
F32 = jnp.float32
BF16 = jnp.bfloat16
VMEM = pl.BlockSpec(memory_space=pltpu.VMEM)


def split(x):
    high = x.astype(BF16)
    return high, (x - high.astype(F32)).astype(BF16)


def iota(shape, dim):
    return lax.broadcasted_iota(jnp.int32, shape, dim)


def dot(a, b):
    return jnp.dot(a, b, preferred_element_type=F32)


def fold(x):
    return jnp.where(iota((8, 128), 1) < 64, x[:8], x[8:])


def unfold(x):
    other, left = pltpu.roll(x, 64, 1), iota(x.shape, 1) < 64
    return jnp.concatenate([jnp.where(left, x, other), jnp.where(left, other, x)], axis=0)


def parity(axis):
    return lax.rem(lax.axis_index(axis), 2)


def load_kernel(*refs):
    sources, held, (near_ref, far_ref, sems) = refs[:6], refs[6:12], refs[12:]
    copies = [pltpu.make_async_copy(a, b, sems.at[i]) for i, (a, b) in enumerate(zip(sources, held))]
    for copy in copies:
        copy.start()
    for copy in copies:
        copy.wait()
    odd = parity("tm") == 1
    for p, ref in enumerate(held[:2]):
        for k in range(3):
            rows = pl.ds(2 * (3 * p + k), 2)
            low, high = ref[k, 0:HT, :], ref[k, HT : 2 * HT, :]
            near_ref[rows, :] = jnp.where(odd, low, high)
            far_ref[rows, :] = jnp.where(odd, high, low)


def widen_kernel(theta_ref, tangent_ref, near_ref, far_ref, after_ref, coef_ref, one_ref, two_ref, wide):
    odd = parity("tm") == 1
    wide[...] = jnp.zeros_like(wide)
    for p, ref in enumerate((theta_ref, tangent_ref)):
        for k in range(3):
            pk = 3 * p + k
            near, far = near_ref[2 * pk : 2 * pk + 2, :], far_ref[2 * pk : 2 * pk + 2, :]
            for base in (0, 64):
                wide[base + 8 * pk : base + 8 * pk + 2, :] = jnp.where(odd, near, far)
                wide[base + 8 * pk + 2 : base + 8 * pk + 6, :] = ref[k]
                wide[base + 8 * pk + 6 : base + 8 * pk + 8, :] = jnp.where(odd, far, near)
    turned = wide[...].T
    coef_ref[...] = turned
    low, high = fold(turned[0:HS]), fold(turned[turned.shape[0] - HS :])
    below = parity("cell") == 1
    one_ref[...] = jnp.where(below, low, high)
    two_ref[...] = jnp.where(below, high, low)


def basis_kernel(
    sfirst_ref, sweight_ref, cov_any, counts_any,
    shigh_ref, slow_ref, turned_high_ref, turned_low_ref, edge_ref, cov_ref, counts_ref, sems,
):
    copies = (pltpu.make_async_copy(cov_any, cov_ref, sems.at[0]), pltpu.make_async_copy(counts_any, counts_ref, sems.at[1]))
    for copy in copies:
        copy.start()
    rows = turned_high_ref.shape[1]
    offset = lax.axis_index("cell") * rows - HS
    first = sfirst_ref[...] - offset
    cells = first.shape[1]
    blocks = []
    for start in range(0, rows + 2 * HS, 32):
        diffs = iota((32, cells), 0) + start - first
        total = jnp.zeros((32, cells), F32)
        for index in range(sweight_ref.shape[0]):
            total = jnp.where(diffs == index, sweight_ref[index : index + 1, :], total)
        high, low = split(total)
        shigh_ref[start : start + 32, :] = high
        slow_ref[start : start + 32, :] = low
        blocks.append(total)
    space = jnp.concatenate(blocks, axis=0)
    turned_high_ref[...], turned_low_ref[...] = split(space[HS : HS + rows].T)
    edge = jnp.concatenate([space[:HS], space[HS + rows :]], axis=0)
    edge_all = jnp.concatenate([edge, edge, edge, jnp.zeros_like(edge)], axis=0).T
    edge_high, edge_low = split(edge_all)
    part = iota(edge_all.shape, 1) // 32
    edge_ref[...] = jnp.where(part == 1, edge_low.astype(F32), edge_high.astype(F32)).astype(BF16)
    for copy in copies:
        copy.wait()


def inner_kernel(coef_ref, high_ref, low_ref, tfirst_ref, tweight_ref, main_ref, spread_ref, gather_ref):
    coef_high, coef_low = split(coef_ref[...])
    main_ref[...] = dot(high_ref[...], coef_high) + dot(low_ref[...], coef_high) + dot(high_ref[...], coef_low)
    tfirst = tfirst_ref[...] - (lax.axis_index("tm") * 4 - HT)
    hours = tfirst.shape[1]
    row = iota((192, hours), 0)
    diffs = row % 8 - tfirst
    total = jnp.zeros((192, hours), F32)
    for index in range(tweight_ref.shape[0]):
        total = jnp.where(diffs == index, tweight_ref[index : index + 1, :], total)
    high, low = split(total)
    high, low = high.astype(F32), low.astype(F32)
    spread = jnp.where(row < 128, high, low)
    owner = (row // 8) % 8
    turned = jnp.where(row[:128] < 64, high[:128], low[:128]).T
    lane = (iota(turned.shape, 1) // 8) % 8
    for pk in range(6):
        mine = jnp.where(owner == pk, spread, 0.0).astype(BF16)
        back = jnp.where(lane == pk, turned, 0.0).astype(BF16)
        for j in range(4):
            spread_ref[j, :, 128 * pk : 128 * pk + 128] = mine[:, 128 * j : 128 * j + 128]
            gather_ref[j, 128 * pk : 128 * pk + 128, :] = back[128 * j : 128 * j + 128, :]


def main_kernel(
    main_ref, first_ref, two_ref, third_ref, edge_ref, spread_ref, gather_ref, shigh_ref, slow_ref, cov_ref, counts_ref,
    own_ref, send_one_ref, send_two_ref, fields, weighted, sums,
):
    odd = parity("cell") == 1
    one = jnp.where(lax.axis_index("cell") < 2, first_ref[...], third_ref[...])
    one, two = unfold(one), unfold(two_ref[...])
    halo = jnp.concatenate([jnp.where(odd, one, two), jnp.where(odd, two, one)], axis=0)
    halo_high, halo_low = split(halo)
    stacked = jnp.concatenate([halo_high, halo_high, halo_low, jnp.zeros_like(halo_low)], axis=0)
    spatial = main_ref[...] + dot(edge_ref[...], stacked)
    high = spatial.astype(BF16).astype(F32)
    left = iota(spatial.shape, 1) < 64
    factor = jnp.concatenate(
        [jnp.where(left, high, spatial - high).astype(BF16), jnp.where(left, high, 0.0).astype(BF16)[:, :64]], axis=1
    )

    cells = fields.shape[1]

    def forward(j):
        fields[j] = dot(factor, spread_ref[j])

    def weigh(j):
        lanes = slice(128 * j, 128 * j + 128)
        for start in range(0, cells, 16):
            rows = slice(start, start + 16)
            lower_rows = slice(cells + start, cells + start + 16)
            cov = [cov_ref[k, rows, lanes] for k in range(3)]
            at = [fields[j, rows, 128 * pk : 128 * pk + 128] for pk in range(6)]
            rates = jnp.exp(cov[0] * at[0] + cov[1] * at[1] + cov[2] * at[2])
            slope = rates * (cov[0] * at[3] + cov[1] * at[4] + cov[2] * at[5])
            excess = counts_ref[rows, lanes].astype(F32) - rates
            for p, value in enumerate((slope, excess)):
                for k in range(3):
                    columns = slice(128 * (3 * p + k), 128 * (3 * p + k) + 128)
                    weighted[j, rows, columns], weighted[j, lower_rows, columns] = split(cov[k] * value)

    def back(j):
        both = dot(weighted[j], gather_ref[j])
        return both[:cells] + both[cells:]

    forward(0)
    total = jnp.zeros(spatial.shape, F32)
    for j in range(4):
        if j < 3:
            forward(j + 1)
        weigh(j)
        if j > 0:
            total = total + back(j - 1)
    total = total + back(3)
    total_high, total_low = split(total)
    whole = dot(shigh_ref[...], jnp.concatenate([total_high, total_low], axis=1))
    summed = whole[:, :128] + whole[:, 128:] + dot(slow_ref[...], total_high)
    summed = summed + pltpu.roll(summed, 64, 1)
    count = own_ref.shape[0]
    own_ref[...] = summed[HS : HS + count]
    low, high = fold(summed[:HS]), fold(summed[HS + count :])
    send_one_ref[...] = jnp.where(odd, low, high)
    send_two_ref[...] = jnp.where(odd, high, low)


def turn_kernel(own_ref, first_ref, two_ref, third_ref, wide_ref, near_ref, far_ref):
    below = parity("cell") == 1
    one = jnp.where(lax.axis_index("cell") < 2, first_ref[...], third_ref[...])
    one, two = unfold(one), unfold(two_ref[...])
    count = own_ref.shape[0]
    low = own_ref[:HS] + jnp.where(below, one, two)
    high = own_ref[count - HS :] + jnp.where(below, two, one)
    turned = jnp.concatenate([low, own_ref[HS : count - HS], high], axis=0).T
    wide_ref[...] = turned[:48]
    odd = parity("tm") == 1
    for pk in range(6):
        low, high = turned[8 * pk : 8 * pk + 2], turned[8 * pk + 6 : 8 * pk + 8]
        near_ref[2 * pk : 2 * pk + 2, :] = jnp.where(odd, low, high)
        far_ref[2 * pk : 2 * pk + 2, :] = jnp.where(odd, high, low)


def finish_kernel(wide_ref, near_ref, far_ref, hess_ref, grad_ref, *, scales):
    odd = parity("tm") == 1
    for p, ref in enumerate((hess_ref, grad_ref)):
        for k in range(3):
            pk = 3 * p + k
            near, far = near_ref[2 * pk : 2 * pk + 2, :], far_ref[2 * pk : 2 * pk + 2, :]
            ref[k, 0:2, :] = (wide_ref[8 * pk + 2 : 8 * pk + 4, :] + jnp.where(odd, near, far)) * scales[p]
            ref[k, 2:4, :] = (wide_ref[8 * pk + 4 : 8 * pk + 6, :] + jnp.where(odd, far, near)) * scales[p]


def call(kernel, outs, scratch=(), final=False, apart=()):
    shape = jax.ShapeDtypeStruct if final else pltpu.VMEM

    def run(*args):
        places = [pl.BlockSpec(memory_space=pltpu.HBM) if i in apart else VMEM for i in range(len(args))]
        return pl.pallas_call(
            kernel,
            out_shape=tuple(shape(s, d) for s, d in outs),
            in_specs=places,
            out_specs=tuple(VMEM for _ in outs),
            scratch_shapes=list(scratch),
            compiler_params=pltpu.CompilerParams(vmem_limit_bytes=24 << 20),
        )(*(pltpu.with_memory_space_constraint(a, pltpu.HBM if i in apart else pltpu.VMEM) for i, a in enumerate(args)))

    return run


def body(theta, tangent, covariates, counts, sfirst, sweight, tfirst, tweight):
    hours = counts.shape[1]
    rows = theta.shape[1]
    cells = counts.shape[0]
    periods, regions = lax.axis_size("tm"), lax.axis_size("cell")

    every = [(t, c) for t in range(periods) for c in range(regions)]

    def swap(value, partner):
        return lax.ppermute(value, ("tm", "cell"), [(t * regions + c, partner(t, c)) for t, c in every])

    def far_of(t, c):
        if t in (0, periods - 1):
            return t * regions + (c ^ 1)
        return (t + 1 if t % 2 else t - 1) * regions + c

    def two_of(t, c):
        if c in (0, regions - 1):
            return (t ^ 1) * regions + c
        return t * regions + (c + 1 if c % 2 else c - 1)

    def over_tm(near, far):
        far = swap(far, far_of)
        near = swap(near, lambda t, c: (t ^ 1) * regions + c)
        return near, far

    def side_of(first):
        return lambda t, c: t * regions + (c ^ 1) if (c < regions // 2) == first else (t ^ 1) * regions + c

    def over_cell_in_three(one, two):
        low = swap(one, side_of(True))
        two = swap(two, two_of)
        high = swap(one, side_of(False))
        return low, two, high

    small = (jnp.swapaxes(theta, 1, 2), jnp.swapaxes(tangent, 1, 2), sfirst[None], sweight, tfirst[None], tweight)
    strip = ((12, rows), F32)
    band = ((HS // 2, 128), F32)
    theta_t, tangent_t, *support, near, far = call(
        load_kernel, [(a.shape, a.dtype) for a in small] + [strip, strip], [pltpu.SemaphoreType.DMA((6,))], apart=range(6)
    )(*small)
    near, far = over_tm(near, far)
    span = rows + 2 * HS
    shigh, slow, turned_high, turned_low, edge, covariates, counts = call(
        basis_kernel,
        [
            ((span, cells), BF16), ((span, cells), BF16), ((cells, rows), BF16), ((cells, rows), BF16), ((cells, 128), BF16),
            (covariates.shape, F32), (counts.shape, counts.dtype),
        ],
        [pltpu.SemaphoreType.DMA((2,))],
        apart=(2, 3),
    )(*support[:2], covariates, counts)
    coef, one, two = call(widen_kernel, [((rows, 128), F32), band, band], [pltpu.VMEM((128, rows), F32)])(
        theta_t, tangent_t, near, far, edge
    )
    low, two, high = over_cell_in_three(one, two)
    main, spread, gather = call(inner_kernel, [((cells, 128), F32), ((4, 192, 768), BF16), ((4, 768, 128), BF16)])(
        coef, turned_high, turned_low, *support[2:]
    )
    own, one, two = call(
        main_kernel,
        [((rows, 128), F32), band, band],
        [pltpu.VMEM((4, cells, 768), F32), pltpu.VMEM((4, 2 * cells, 768), BF16), pltpu.VMEM((cells, 128), F32)],
    )(main, low, two, high, edge, spread, gather, shigh, slow, covariates, counts)
    low, two, high = over_cell_in_three(one, two)
    wide, near, far = call(turn_kernel, [((48, rows), F32), strip, strip])(own, low, two, high)
    near, far = over_tm(near, far)
    scales = (1.0 / (16 * (hours // 4)), 1.0 / (hours // 4))

    def last(*refs):
        finish_kernel(*refs, scales=scales)

    hess, grad = call(last, [((3, 4, rows), F32)] * 2, final=True)(wide, near, far)
    return jnp.swapaxes(hess, 1, 2), jnp.swapaxes(grad, 1, 2)


def solution(mesh):
    return jax.shard_map(
        body,
        mesh=mesh,
        in_specs=(
            P(None, "cell", "tm"),
            P(None, "cell", "tm"),
            P(None, "cell", "tm"),
            P("cell", "tm"),
            P("cell"),
            P(None, "cell"),
            P("tm"),
            P(None, "tm"),
        ),
        out_specs=(P(None, "cell", "tm"), P(None, "cell", "tm")),
        check_vma=False,
    )
```
